256 devices in a mesh: cells: 64 (over z, y_hi, x), genes: 4 (over y_lo, core).
Axes of the slice: x: 4, y: 4 (y_hi: 2, y_lo: 2; y = y_hi * 2 + y_lo), z: 8, core: 2. Of those that a mesh axis runs over, the one named last changes fastest.
Arguments:
- counts: int32 [2000, 393216], P('genes', 'cells'), may hold values from 0 to 21, as said below
- start_basis: float32 [2000, 64], P('genes'), may hold values from -6 to 6
Outputs:
- embeddings: float32 [393216, 64], P(('cells', 'genes'))
The draws below stay inside these ranges and needn't reach their ends.
Inputs may be any that keep to these rules, and one draw needn't show every extreme that they name: `counts`: every cell has at least one nonzero count.
All inputs are finite; a program needn't handle non-finite values.
Results may differ from the reference program's by a relative error of at most 0.00015.
Values sent between devices are 32-bit elements; how exact they have to be, the bound alone decides.
No kernel may reach another device: no remote copies, remote signals or barrier semaphores. Data moves between devices by JAX's collectives and lax.ppermute only.
A program may use at most 128 MiB of HBM per device.

```python
import math
import jax
import jax.numpy as jnp
from jax import lax

G = 2000
R = 64
ITERS = 2
C_DEV = 6144
CELLS = 393216


def draw_counts(key, part):
    key_rate, key_depth, key_present, key_value, key_forced = jax.random.split(key, 5)
    gene_ids = jnp.arange(G, dtype=jnp.int32)
    cell_ids = jnp.arange(CELLS, dtype=jnp.int32)
    set_cells = CELLS // 2
    position = cell_ids % set_cells
    rate_code = jax.random.randint(key_rate, (G,), 2, 9, dtype=jnp.int32) + 4 * gene_ids // G
    threshold = jnp.left_shift(jnp.ones((G,), jnp.int32), rate_code)
    depth_top = 3 + 8 * position // set_cells
    depth = jax.random.randint(key_depth, (CELLS,), 1, depth_top + 1, dtype=jnp.int32)
    uniform_draw = jax.random.randint(key_present, (G, CELLS), 0, 4096, dtype=jnp.int32)
    values = 1 + jax.random.randint(key_value, (G, CELLS), 0, 2 * depth[None, :], dtype=jnp.int32)
    present = uniform_draw < threshold[:, None] * depth[None, :]
    forced = jax.random.randint(key_forced, (CELLS,), 0, G, dtype=jnp.int32)
    extra = (gene_ids[:, None] == forced[None, :]).astype(jnp.int32)
    return jnp.where(present, values, 0) + extra


def levels(key, dims, cuts, low, top_value):
    def one(dim, parts):
        draws = jax.random.uniform(jax.random.fold_in(jax.random.fold_in(key, 6), dim), (parts,), jnp.float32, low / len(cuts), top_value / len(cuts))
        return jnp.repeat(jnp.exp(draws), dims[dim] // parts).reshape((-1,) + (1,) * (len(dims) - dim - 1))

    factor_of = one(*cuts[0])
    for cut in cuts[1:]:
        factor_of = factor_of * one(*cut)
    return factor_of


def noise(stream_key, dims, scale, most, cuts=(), kind=jnp.bfloat16):
    gain = levels(stream_key, dims, cuts, -0.22, 0.18) if cuts else 1.0
    array = jax.random.normal(stream_key, dims, jnp.float32) * scale * gain
    return jnp.minimum(jnp.maximum(array, -most), most).astype(kind)


def setup_inputs(seed: int = 0) -> dict:
    splits = jax.random.split(jax.random.key(seed), 3)
    return {
        "counts": draw_counts(jax.random.fold_in(splits[2], 71), 0),
        "start_basis": noise(splits[1], (G, R), 1.0, 6.0, ((0, 4),), jnp.float32),
    }


epsilon = 1e-05
clip_top = 10.0
highest = lax.Precision.HIGHEST

def orthonormal(matrix):
    gram_set = jnp.dot(matrix.T, matrix, precision=highest)
    factor = jnp.linalg.cholesky(gram_set)
    return jax.scipy.linalg.solve_triangular(factor, matrix.T, lower=True).T

def reference(counts, start_basis):
    gene_count, total_cells = counts.shape
    rank_cols = start_basis.shape[1]
    set_cells = total_cells // 2
    block_cols = C_DEV
    per_set = set_cells // block_cols

    def raw_block(index):
        return lax.dynamic_slice_in_dim(counts, index * block_cols, block_cols, 1).astype(jnp.float32)
    totals = lax.map(lambda index: lax.optimization_barrier(jnp.sum(raw_block(index), axis=0)), jnp.arange(2 * per_set, dtype=jnp.int32))

    def log_block(index):
        return jnp.log1p(10000.0 * raw_block(index) / totals[index][None, :])

    def set_sum(dataset, fn, init):

        def sweep(carried, inner):
            return (carried + fn(dataset * per_set + inner, inner), None)
        return lax.scan(sweep, init, jnp.arange(per_set, dtype=jnp.int32))[0]
    zero_genes = jnp.zeros((gene_count,), jnp.float32)
    centers = []
    deviations = []
    for dataset in range(2):
        center = set_sum(dataset, lambda index, inner: lax.optimization_barrier(jnp.sum(log_block(index), axis=1)), zero_genes) / set_cells
        spread = set_sum(dataset, lambda index, inner: lax.optimization_barrier(jnp.sum(jnp.square(log_block(index) - center[:, None]), axis=1)), zero_genes) / set_cells
        centers.append(center)
        deviations.append(jnp.sqrt(spread + epsilon))

    def scaled_block(dataset, index):
        return jnp.minimum((log_block(index) - centers[dataset][:, None]) / deviations[dataset][:, None], clip_top)

    def project(dataset, weight):

        def one_block(inner):
            return lax.dot_general(scaled_block(dataset, dataset * per_set + inner), weight, (((0,), (0,)), ((), ())), precision=highest)
        pieces = lax.map(one_block, jnp.arange(per_set, dtype=jnp.int32))
        return pieces.reshape(set_cells, rank_cols)

    def product(dataset, basis):

        def one_block(index, inner):
            rows_here = lax.dynamic_slice_in_dim(basis, inner * block_cols, block_cols, 0)
            return jnp.dot(scaled_block(dataset, index), rows_here, precision=highest)
        return set_sum(dataset, one_block, jnp.zeros((gene_count, rank_cols), jnp.float32))
    bases = [orthonormal(project(0, start_basis)), orthonormal(project(1, start_basis))]
    for sweep_index in range(ITERS):
        products = [product(0, bases[0]), product(1, bases[1])]
        bases = [orthonormal(project(0, products[1])), orthonormal(project(1, products[0]))]
    return jnp.concatenate(bases, axis=0) * math.sqrt(set_cells)
```

```python
import math

import jax
import jax.numpy as jnp
from jax import lax
from jax.sharding import PartitionSpec as P

ITERS = 2


epsilon = 1e-05
clip_top = 10.0
highest = lax.Precision.HIGHEST


def swapped(value, axis, mask):
    return lax.ppermute(value, axis, [(s, s ^ mask) for s in range(lax.axis_size(axis))])


def halves(axis):
    size = lax.axis_size(axis)
    return [list(range(size // 2)), list(range(size // 2, size))]


def alike(axis, bits):
    size = lax.axis_size(axis)
    groups = {}
    for index in range(size):
        groups.setdefault(index & ~bits, []).append(index)
    return list(groups.values())


def over_group(value, axis, bits):
    shards = lax.all_gather(value, axis, axis_index_groups=alike(axis, bits))
    return shards.sum(axis=0)


def split(value):
    upper = lax.reduce_precision(value, 8, 7)
    lower = lax.reduce_precision(value - upper, 8, 7)
    return upper.astype(jnp.bfloat16), lower.astype(jnp.bfloat16)


def in_parts(left, upper, lower, dim):
    first, second = split(left)
    rank = left.shape[0]

    def dot(a, b):
        return lax.dot_general(a, b, (((1,), (dim,)), ((), ())), preferred_element_type=jnp.float32)

    wide = dot(jnp.concatenate([first, second]), upper)
    return wide[:rank] + (wide[rank:] + dot(first, lower))


def gram_of(rows_t):
    return lax.dot_general(rows_t, rows_t, (((1,), (1,)), ((), ())), precision=highest)


def inverse_factor(gram):
    factor = jnp.linalg.cholesky(gram)
    return jax.scipy.linalg.solve_triangular(factor, jnp.eye(len(gram), dtype=gram.dtype), lower=True)


def shards(counts, start_basis):
    genes_dev, cells_dev = counts.shape
    rank = start_basis.shape[1]
    cell_devs = lax.axis_size("cells")
    half_devs = cell_devs // 2
    set_cells = cells_dev * half_devs
    share = cells_dev // lax.axis_size("genes")
    other_half = 1 - lax.axis_index("cells") // half_devs
    core = lax.axis_index("genes") % 2
    side = lax.axis_index("genes") // 2

    def to_half(pieces):
        return lax.all_to_all(
            pieces, "cells", 0, 0, axis_index_groups=halves("cells"), tiled=True
        )

    raw_counts = counts.astype(jnp.float32)
    totals = lax.all_gather(jnp.sum(raw_counts, axis=0)[None], "genes", tiled=True).sum(axis=0)
    lognorm = jnp.log(1.0 + raw_counts * (10000.0 / totals)[None, :])

    sums = jnp.stack([jnp.sum(lognorm, axis=1), jnp.sum(lognorm * lognorm, axis=1)])
    sums = to_half(jnp.broadcast_to(sums, (half_devs, 2, genes_dev))).sum(axis=0)
    center = sums[0] / set_cells
    spread = sums[1] / set_cells - center * center
    scale = 1.0 / jnp.sqrt(spread + epsilon)
    scaled = jnp.minimum((lognorm - center[:, None]) * scale[:, None], clip_top)
    upper, lower = split(scaled)

    def project(weight_t):
        return in_parts(weight_t, upper, lower, 0)

    def exchanged(first, second):
        mine = jnp.where(core == 0, first, second)
        sent = jnp.where(core == 0, second, first)
        return mine + swapped(sent, "genes", 1)

    def product(proj):
        partial = in_parts(proj, upper, lower, 1)
        own = to_half(partial.reshape(half_devs, rank // half_devs, genes_dev)).sum(axis=0)
        everywhere = lax.all_to_all(
            jnp.broadcast_to(own, (cell_devs, *own.shape)), "cells", 0, 0, tiled=True
        )
        theirs = lax.dynamic_slice_in_dim(everywhere, other_half * half_devs, half_devs, 0)
        return theirs.reshape(rank, genes_dev)

    weight_t = start_basis.T
    inverse = None
    for sweep in range(ITERS):
        partial = project(weight_t)
        half = exchanged(partial[:, : 2 * share], partial[:, 2 * share :])
        half = half + swapped(half, "genes", 2)
        if inverse is not None:
            half = jnp.dot(inverse, half, precision=highest)
        twin = swapped(half, "genes", 1)
        first, second = jnp.where(core == 0, half, twin), jnp.where(core == 0, twin, half)
        weight_t = product(jnp.concatenate([first, second], axis=1))
        inverse = inverse_factor(lax.all_gather(gram_of(weight_t), "genes").sum(axis=0))

    partial = project(weight_t)
    blocks = [partial[:, b * share : (b + 1) * share] for b in range(4)]
    half = exchanged(
        jnp.concatenate([blocks[0], blocks[2]], axis=1), jnp.concatenate([blocks[1], blocks[3]], axis=1)
    )
    mine = jnp.where(side == 0, half[:, :share], half[:, share:])
    sent = jnp.where(side == 0, half[:, share:], half[:, :share])
    rows = jnp.dot(inverse, mine + swapped(sent, "genes", 2), precision=highest)
    gram = lax.all_gather(gram_of(rows), "genes").sum(axis=0)
    gram = over_group(gram, "cells", 3)
    gram = over_group(gram, "cells", 24)
    gram = gram + swapped(gram, "cells", 4)
    final = jnp.dot(inverse_factor(gram), rows, precision=highest)
    return final.T * math.sqrt(set_cells)


def solution(mesh):
    placed = (P("genes", "cells"), P("genes", None))
    return jax.shard_map(
        shards, mesh=mesh, in_specs=placed, out_specs=P(("cells", "genes"), None), check_vma=False
    )
```

```python
import math

import jax
import jax.numpy as jnp
from jax import lax
from jax.experimental import pallas as pl
from jax.experimental.pallas import tpu as pltpu
from jax.sharding import PartitionSpec as P

ITERS = 2


epsilon = 1e-05
clip_top = 10.0
highest = lax.Precision.HIGHEST


def swapped(value, axis, mask):
    return lax.ppermute(value, axis, [(s, s ^ mask) for s in range(lax.axis_size(axis))])


def halves(axis):
    size = lax.axis_size(axis)
    return [list(range(size // 2)), list(range(size // 2, size))]


def over_four(value, axis, low, high):
    first = value + swapped(value, axis, low)
    return first + (swapped(value, axis, high) + swapped(value, axis, low | high))


def over_half(value):
    value = over_four(value, "cells", 1, 2)
    value = over_four(value, "cells", 8, 16)
    return value + swapped(value, "cells", 4)


def split(value):
    upper = lax.reduce_precision(value, 8, 7)
    lower = lax.reduce_precision(value - upper, 8, 7)
    return upper.astype(jnp.bfloat16), lower.astype(jnp.bfloat16)


def in_parts(left, upper, lower, dim):
    first, second = split(left)
    rank = left.shape[0]

    def dot(a, b):
        return lax.dot_general(a, b, (((1,), (dim,)), ((), ())), preferred_element_type=jnp.float32)

    wide = dot(jnp.concatenate([first, second]), upper)
    return wide[:rank] + (wide[rank:] + dot(first, lower))


def gram_of(rows_t):
    return lax.dot_general(rows_t, rows_t, (((1,), (1,)), ((), ())), precision=highest)


def inverse_factor_kernel(gram_ref, out_ref):
    size = gram_ref.shape[0]
    tiles = size // 8
    lane = lax.broadcasted_iota(jnp.int32, (8, 2 * size), 1)
    line = lax.broadcasted_iota(jnp.int32, (8, 2 * size), 0)
    gram = gram_ref[...]
    both = jnp.concatenate([gram, jnp.zeros_like(gram)], axis=1)
    rows = [
        jnp.where(lane == line + (size + 8 * t), 1.0, both[8 * t : 8 * t + 8]) for t in range(tiles)
    ]
    for k in range(size):
        t, r = divmod(k, 8)
        columns = [
            jnp.broadcast_to(rows[u][:, k : k + 1], (8, 2 * size)) for u in range(t, tiles)
        ]
        unit = (rows[t] / columns[0])[r : r + 1]
        pivot = jnp.broadcast_to(unit, (8, 2 * size))
        for u in range(t, tiles):
            column = columns[u - t]
            if u == t:
                column = jnp.where(line > r, column, 0.0)
            rows[u] = rows[u] - column * pivot
    for t in range(tiles):
        diagonal = jnp.sum(jnp.where(lane == line + 8 * t, rows[t], 0.0), axis=1, keepdims=True)
        out_ref[8 * t : 8 * t + 8] = rows[t][:, size:] / jnp.sqrt(diagonal)


def inverse_factor(gram):
    return pl.pallas_call(
        inverse_factor_kernel,
        out_shape=jax.ShapeDtypeStruct(gram.shape, gram.dtype),
        in_specs=[pl.BlockSpec(memory_space=pltpu.VMEM)],
        out_specs=pl.BlockSpec(memory_space=pltpu.VMEM),
        compiler_params=pltpu.CompilerParams(vmem_limit_bytes=1 << 20),
        cost_estimate=pl.CostEstimate(flops=1 << 20, bytes_accessed=1 << 15, transcendentals=128),
        name="inverse_factor",
    )(gram)


def shards(counts, start_basis):
    genes_dev, cells_dev = counts.shape
    rank = start_basis.shape[1]
    cell_devs = lax.axis_size("cells")
    half_devs = cell_devs // 2
    set_cells = cells_dev * half_devs
    share = cells_dev // lax.axis_size("genes")
    other_half = 1 - lax.axis_index("cells") // half_devs
    core = lax.axis_index("genes") % 2
    side = lax.axis_index("genes") // 2

    def to_half(pieces):
        return lax.all_to_all(
            pieces, "cells", 0, 0, axis_index_groups=halves("cells"), tiled=True
        )

    raw_counts = counts.astype(jnp.float32)
    totals = lax.all_gather(jnp.sum(raw_counts, axis=0)[None], "genes", tiled=True).sum(axis=0)
    lognorm = jnp.log(1.0 + raw_counts * (10000.0 / totals)[None, :])

    sums = jnp.stack([jnp.sum(lognorm, axis=1), jnp.sum(lognorm * lognorm, axis=1)])
    sums = over_half(sums)
    center = sums[0] / set_cells
    spread = sums[1] / set_cells - center * center
    scale = 1.0 / jnp.sqrt(spread + epsilon)
    scaled = jnp.minimum((lognorm - center[:, None]) * scale[:, None], clip_top)
    upper, lower = split(scaled)

    def project(weight_t):
        return in_parts(weight_t, upper, lower, 0)

    def exchanged(first, second):
        mine = jnp.where(core == 0, first, second)
        sent = jnp.where(core == 0, second, first)
        return mine + swapped(sent, "genes", 1)

    def product(proj):
        partial = in_parts(proj, upper, lower, 1)
        own = to_half(partial.reshape(half_devs, rank // half_devs, genes_dev)).sum(axis=0)
        everywhere = lax.all_to_all(
            jnp.broadcast_to(own, (cell_devs, *own.shape)), "cells", 0, 0, tiled=True
        )
        theirs = lax.dynamic_slice_in_dim(everywhere, other_half * half_devs, half_devs, 0)
        return theirs.reshape(rank, genes_dev)

    def over_genes_inverse(weight_t):
        return inverse_factor(lax.all_gather(gram_of(weight_t), "genes").sum(axis=0))

    weight_t = start_basis.T
    for sweep in range(ITERS):
        partial = project(weight_t)
        half = exchanged(partial[:, : 2 * share], partial[:, 2 * share :])
        if sweep:
            half, weight_t = lax.optimization_barrier((half, weight_t))
            inverse = over_genes_inverse(weight_t)
        half = half + swapped(half, "genes", 2)
        if sweep:
            half = jnp.dot(inverse, half, precision=highest)
        twin = swapped(half, "genes", 1)
        first, second = jnp.where(core == 0, half, twin), jnp.where(core == 0, twin, half)
        weight_t = product(jnp.concatenate([first, second], axis=1))

    partial = project(weight_t)
    blocks = [partial[:, b * share : (b + 1) * share] for b in range(4)]
    half = exchanged(
        jnp.concatenate([blocks[0], blocks[2]], axis=1), jnp.concatenate([blocks[1], blocks[3]], axis=1)
    )
    half, weight_t = lax.optimization_barrier((half, weight_t))
    inverse = over_genes_inverse(weight_t)
    mine = jnp.where(side == 0, half[:, :share], half[:, share:])
    sent = jnp.where(side == 0, half[:, share:], half[:, :share])
    rows = jnp.dot(inverse, mine + swapped(sent, "genes", 2), precision=highest)
    gram = over_half(lax.all_gather(gram_of(rows), "genes").sum(axis=0))
    final = jnp.dot(inverse_factor(gram), rows, precision=highest)
    return final.T * math.sqrt(set_cells)


def solution(mesh):
    placed = (P("genes", "cells"), P("genes", None))
    return jax.shard_map(
        shards, mesh=mesh, in_specs=placed, out_specs=P(("cells", "genes"), None), check_vma=False
    )
```

```python
import math

import jax
import jax.numpy as jnp
from jax import lax
from jax.experimental import pallas as pl
from jax.experimental.layout import Layout, with_layout_constraint
from jax.experimental.pallas import tpu as pltpu
from jax.sharding import PartitionSpec as P

ITERS = 2


epsilon = 1e-05
clip_top = 10.0
highest = lax.Precision.HIGHEST


def swapped(value, axis, mask):
    return lax.ppermute(value, axis, [(s, s ^ mask) for s in range(lax.axis_size(axis))])


def over_four(value, axis, low, high):
    first = value + swapped(value, axis, low)
    return first + (swapped(value, axis, high) + swapped(value, axis, low | high))


def over_half(value):
    value = over_four(value, "cells", 1, 2)
    value = over_four(value, "cells", 8, 16)
    return value + swapped(value, "cells", 4)


def split(value):
    upper = lax.reduce_precision(value, 8, 7)
    lower = lax.reduce_precision(value - upper, 8, 7)
    return upper.astype(jnp.bfloat16), lower.astype(jnp.bfloat16)


def in_parts(left, upper, lower, dim):
    first, second = split(left)
    rank = left.shape[0]

    def dot(a, b):
        return lax.dot_general(a, b, (((1,), (dim,)), ((), ())), preferred_element_type=jnp.float32)

    wide = dot(jnp.concatenate([first, second]), upper)
    return wide[:rank] + (wide[rank:] + dot(first, lower))


def in_rows(value):
    return with_layout_constraint(value, Layout(major_to_minor=(0, 1)))


def gram_of(rows_t):
    return lax.dot_general(rows_t, rows_t, (((1,), (1,)), ((), ())), precision=highest)


def inverse_factor_kernel(gram_ref, out_ref):
    size = gram_ref.shape[0]
    tiles = size // 8
    lane = lax.broadcasted_iota(jnp.int32, (8, 2 * size), 1)
    line = lax.broadcasted_iota(jnp.int32, (8, 2 * size), 0)
    gram = gram_ref[...]
    both = jnp.concatenate([gram, jnp.zeros_like(gram)], axis=1)
    rows = [
        jnp.where(lane == line + (size + 8 * t), 1.0, both[8 * t : 8 * t + 8]) for t in range(tiles)
    ]
    for k in range(size):
        t, r = divmod(k, 8)
        columns = [
            jnp.broadcast_to(rows[u][:, k : k + 1], (8, 2 * size)) for u in range(t, tiles)
        ]
        unit = (rows[t] / columns[0])[r : r + 1]
        pivot = jnp.broadcast_to(unit, (8, 2 * size))
        for u in range(t, tiles):
            column = columns[u - t]
            if u == t:
                column = jnp.where(line > r, column, 0.0)
            rows[u] = rows[u] - column * pivot
    for t in range(tiles):
        diagonal = jnp.sum(jnp.where(lane == line + 8 * t, rows[t], 0.0), axis=1, keepdims=True)
        out_ref[8 * t : 8 * t + 8] = rows[t][:, size:] / jnp.sqrt(diagonal)


def inverse_factor(gram):
    return pl.pallas_call(
        inverse_factor_kernel,
        out_shape=jax.ShapeDtypeStruct(gram.shape, gram.dtype),
        in_specs=[pl.BlockSpec(memory_space=pltpu.VMEM)],
        out_specs=pl.BlockSpec(memory_space=pltpu.VMEM),
        compiler_params=pltpu.CompilerParams(vmem_limit_bytes=1 << 20),
        cost_estimate=pl.CostEstimate(flops=1 << 20, bytes_accessed=1 << 15, transcendentals=128),
        name="inverse_factor",
    )(gram)


def shards(counts, start_basis):
    genes_dev, cells_dev = counts.shape
    rank = start_basis.shape[1]
    half_devs = lax.axis_size("cells") // 2
    set_cells = cells_dev * half_devs
    share = cells_dev // lax.axis_size("genes")
    core = lax.axis_index("genes") % 2
    side = lax.axis_index("genes") // 2

    raw_counts = counts.astype(jnp.float32)
    totals = lax.all_gather(jnp.sum(raw_counts, axis=0)[None], "genes", tiled=True).sum(axis=0)
    lognorm = jnp.log(1.0 + raw_counts * (10000.0 / totals)[None, :])

    sums = jnp.stack([jnp.sum(lognorm, axis=1), jnp.sum(lognorm * lognorm, axis=1)])
    sums = over_half(sums)
    center = sums[0] / set_cells
    spread = sums[1] / set_cells - center * center
    scale = 1.0 / jnp.sqrt(spread + epsilon)
    scaled = jnp.minimum((lognorm - center[:, None]) * scale[:, None], clip_top)
    upper, lower = split(scaled)

    def project(weight_t):
        return in_parts(weight_t, upper, lower, 0)

    def exchanged(first, second):
        mine = jnp.where(core == 0, first, second)
        sent = jnp.where(core == 0, second, first)
        return mine + swapped(sent, "genes", 1)

    place = lax.axis_index("cells") % 4
    low, high = place % 2 == 1, place // 2 == 1

    def crossed(pieces):
        a, b, c, d = pieces
        a, b, c, d = jnp.where(low, b, a), jnp.where(low, a, b), jnp.where(low, d, c), jnp.where(low, c, d)
        return jnp.where(high, c, a), jnp.where(high, d, b), jnp.where(high, a, c), jnp.where(high, b, d)

    def product(proj):
        partial = in_rows(in_parts(proj, upper, lower, 1))
        quarter = rank // 4
        kept, *sent = crossed([partial[i * quarter : (i + 1) * quarter] for i in range(4)])
        came = [swapped(piece, "cells", i + 1) for i, piece in enumerate(sent)]
        part = (kept + came[0]) + (came[1] + came[2])
        part = part + swapped(part, "cells", 4)
        came = [swapped(part, "cells", half_devs | mask) for mask in (0, 8, 16, 24)]
        part = (came[0] + came[1]) + (came[2] + came[3])
        came = [swapped(part, "cells", i) for i in (1, 2, 3)]
        return in_rows(jnp.concatenate(crossed([part, *came])))

    weight_t = start_basis.T
    for sweep in range(ITERS):
        if sweep:
            weight_t, gram = lax.optimization_barrier((weight_t, gram_of(weight_t)))
            gram = over_four(gram, "genes", 1, 2)
        partial = project(weight_t)
        half = exchanged(partial[:, : 2 * share], partial[:, 2 * share :])
        if sweep:
            half, gram = lax.optimization_barrier((half, gram))
            inverse = inverse_factor(gram)
        half = half + swapped(half, "genes", 2)
        if sweep:
            half = jnp.dot(inverse, half, precision=highest)
        twin = swapped(half, "genes", 1)
        first, second = jnp.where(core == 0, half, twin), jnp.where(core == 0, twin, half)
        weight_t = product(jnp.concatenate([first, second], axis=1))

    weight_t, gram = lax.optimization_barrier((weight_t, gram_of(weight_t)))
    gram = over_four(gram, "genes", 1, 2)
    partial = project(weight_t)
    blocks = [partial[:, b * share : (b + 1) * share] for b in range(4)]
    half = exchanged(
        jnp.concatenate([blocks[0], blocks[2]], axis=1), jnp.concatenate([blocks[1], blocks[3]], axis=1)
    )
    half, gram = lax.optimization_barrier((half, gram))
    inverse = inverse_factor(gram)
    mine = jnp.where(side == 0, half[:, :share], half[:, share:])
    sent = jnp.where(side == 0, half[:, share:], half[:, :share])
    rows = jnp.dot(inverse, mine + swapped(sent, "genes", 2), precision=highest)
    gram = over_half(over_four(gram_of(rows), "genes", 1, 2))
    final = jnp.dot(inverse_factor(gram), rows, precision=highest)
    return final.T * math.sqrt(set_cells)


def solution(mesh):
    placed = (P("genes", "cells"), P("genes", None))
    return jax.shard_map(
        shards, mesh=mesh, in_specs=placed, out_specs=P(("cells", "genes"), None), check_vma=False
    )
```

```python
import math

import jax
import jax.numpy as jnp
from jax import lax
from jax.experimental import pallas as pl
from jax.experimental.layout import Layout, with_layout_constraint
from jax.experimental.pallas import tpu as pltpu
from jax.sharding import PartitionSpec as P


ITERS = 2


epsilon = 1e-05
clip_top = 10.0
highest = lax.Precision.HIGHEST


def swapped(value, axis, mask):
    return lax.ppermute(value, axis, [(s, s ^ mask) for s in range(lax.axis_size(axis))])


def over_four(value, axis, low, high):
    first = value + swapped(value, axis, low)
    return first + (swapped(value, axis, high) + swapped(value, axis, low | high))


def over_half(value):
    value = over_four(value, "cells", 1, 2)
    value = over_four(value, "cells", 8, 16)
    return value + swapped(value, "cells", 4)


def split(value):
    upper = lax.reduce_precision(value, 8, 7)
    lower = lax.reduce_precision(value - upper, 8, 7)
    return upper.astype(jnp.bfloat16), lower.astype(jnp.bfloat16)


def in_parts(left, upper, lower, dim):
    first, second = split(left)
    rank = left.shape[0]

    def dot(a, b):
        return lax.dot_general(a, b, (((1,), (dim,)), ((), ())), preferred_element_type=jnp.float32)

    wide = dot(jnp.concatenate([first, second]), upper)
    return wide[:rank] + (wide[rank:] + dot(first, lower))


def in_rows(value):
    return with_layout_constraint(value, Layout(major_to_minor=(0, 1)))


def gram_of(rows_t):
    return lax.dot_general(rows_t, rows_t, (((1,), (1,)), ((), ())), precision=highest)


def inverse_factor_kernel(gram_ref, out_ref):
    size = gram_ref.shape[0]
    tiles = size // 8
    lane = lax.broadcasted_iota(jnp.int32, (8, 2 * size), 1)
    line = lax.broadcasted_iota(jnp.int32, (8, 2 * size), 0)
    gram = gram_ref[...]
    both = jnp.concatenate([gram, jnp.zeros_like(gram)], axis=1)
    rows = [
        jnp.where(lane == line + (size + 8 * t), 1.0, both[8 * t : 8 * t + 8]) for t in range(tiles)
    ]
    for k in range(size):
        t, r = divmod(k, 8)
        columns = [
            jnp.broadcast_to(rows[u][:, k : k + 1], (8, 2 * size)) for u in range(t, tiles)
        ]
        unit = (rows[t] / columns[0])[r : r + 1]
        pivot = jnp.broadcast_to(unit, (8, 2 * size))
        for u in range(t, tiles):
            column = columns[u - t]
            if u == t:
                column = jnp.where(line > r, column, 0.0)
            rows[u] = rows[u] - column * pivot
    for t in range(tiles):
        diagonal = jnp.sum(jnp.where(lane == line + 8 * t, rows[t], 0.0), axis=1, keepdims=True)
        out_ref[8 * t : 8 * t + 8] = rows[t][:, size:] / jnp.sqrt(diagonal)


def inverse_factor(gram):
    return pl.pallas_call(
        inverse_factor_kernel,
        out_shape=jax.ShapeDtypeStruct(gram.shape, gram.dtype),
        in_specs=[pl.BlockSpec(memory_space=pltpu.VMEM)],
        out_specs=pl.BlockSpec(memory_space=pltpu.VMEM),
        compiler_params=pltpu.CompilerParams(vmem_limit_bytes=1 << 20),
        cost_estimate=pl.CostEstimate(flops=1 << 20, bytes_accessed=1 << 15, transcendentals=128),
        name="inverse_factor",
    )(gram)


def shards(counts, start_basis):
    _, cells_dev = counts.shape
    rank = start_basis.shape[1]
    half_devs = lax.axis_size("cells") // 2
    set_cells = cells_dev * half_devs
    share = cells_dev // lax.axis_size("genes")
    core = lax.axis_index("genes") % 2
    side = lax.axis_index("genes") // 2

    raw_counts = counts.astype(jnp.float32)
    totals = lax.all_gather(jnp.sum(raw_counts, axis=0)[None], "genes", tiled=True).sum(axis=0)
    lognorm = jnp.log(1.0 + raw_counts * (10000.0 / totals)[None, :])

    sums = jnp.stack([jnp.sum(lognorm, axis=1), jnp.sum(lognorm * lognorm, axis=1)])
    sums = over_half(sums)
    center = sums[0] / set_cells
    spread = sums[1] / set_cells - center * center
    scale = 1.0 / jnp.sqrt(spread + epsilon)
    scaled = jnp.minimum((lognorm - center[:, None]) * scale[:, None], clip_top)
    upper, lower = split(scaled)

    def project(weight_t):
        return in_parts(weight_t, upper, lower, 0)

    def exchanged(first, second):
        mine = jnp.where(core == 0, first, second)
        sent = jnp.where(core == 0, second, first)
        return mine + swapped(sent, "genes", 1)

    mirror = lax.axis_size("cells") - 8
    place = lax.axis_index("cells") % 4
    low, high = place % 2 == 1, place // 2 == 1

    def crossed(pieces):
        a, b, c, d = pieces
        a, b, c, d = jnp.where(low, b, a), jnp.where(low, a, b), jnp.where(low, d, c), jnp.where(low, c, d)
        return jnp.where(high, c, a), jnp.where(high, d, b), jnp.where(high, a, c), jnp.where(high, b, d)

    def product(proj):
        partial = in_rows(in_parts(proj, upper, lower, 1))
        quarter = rank // 4
        sent = crossed([partial[i * quarter : (i + 1) * quarter] for i in range(4)])
        came = [swapped(piece, "cells", mirror | i) for i, piece in enumerate(sent)]
        part = (came[0] + came[1]) + (came[2] + came[3])
        part = part + swapped(part, "cells", 4)
        part = over_four(part, "cells", 8, 16)
        came = [swapped(part, "cells", i) for i in (1, 2, 3)]
        return in_rows(jnp.concatenate(crossed([part, *came])))

    weight_t = start_basis.T
    for sweep in range(ITERS):
        if sweep:
            weight_t, gram = lax.optimization_barrier((weight_t, gram_of(weight_t)))
            gram = over_four(gram, "genes", 1, 2)
        partial = project(weight_t)
        half = exchanged(partial[:, : 2 * share], partial[:, 2 * share :])
        if sweep:
            half, gram = lax.optimization_barrier((half, gram))
            inverse = inverse_factor(gram)
        half = half + swapped(half, "genes", 2)
        if sweep:
            half = jnp.dot(inverse, half, precision=highest)
        twin = swapped(half, "genes", 1)
        first, second = jnp.where(core == 0, half, twin), jnp.where(core == 0, twin, half)
        weight_t = product(jnp.concatenate([first, second], axis=1))

    weight_t, gram = lax.optimization_barrier((weight_t, gram_of(weight_t)))
    gram = over_four(gram, "genes", 1, 2)
    partial = project(weight_t)
    blocks = [partial[:, b * share : (b + 1) * share] for b in range(4)]
    half = exchanged(
        jnp.concatenate([blocks[0], blocks[2]], axis=1), jnp.concatenate([blocks[1], blocks[3]], axis=1)
    )
    half, gram = lax.optimization_barrier((half, gram))
    inverse = inverse_factor(gram)
    mine = jnp.where(side == 0, half[:, :share], half[:, share:])
    sent = jnp.where(side == 0, half[:, share:], half[:, :share])
    rows = jnp.dot(inverse, mine + swapped(sent, "genes", 2), precision=highest)
    gram = over_half(over_four(gram_of(rows), "genes", 1, 2))
    final = jnp.dot(inverse_factor(gram), rows, precision=highest)
    return final.T * math.sqrt(set_cells)


def solution(mesh):
    placed = (P("genes", "cells"), P("genes", None))
    return jax.shard_map(
        shards, mesh=mesh, in_specs=placed, out_specs=P(("cells", "genes"), None), check_vma=False
    )
```

```python
import math

import jax
import jax.numpy as jnp
from jax import lax
from jax.experimental import pallas as pl
from jax.experimental.layout import Layout, with_layout_constraint
from jax.experimental.pallas import tpu as pltpu
from jax.sharding import PartitionSpec as P


epsilon = 1e-05
clip_top = 10.0
highest = lax.Precision.HIGHEST


def swapped(value, axis, mask):
    return lax.ppermute(value, axis, [(s, s ^ mask) for s in range(lax.axis_size(axis))])


def over_four(value, axis, low, high):
    first = value + swapped(value, axis, low)
    return first + (swapped(value, axis, high) + swapped(value, axis, low | high))


def among(pieces, axis, bits):
    groups = {}
    for index in range(lax.axis_size(axis)):
        groups.setdefault(index & ~bits, []).append(index)
    return lax.all_to_all(
        pieces, axis, 0, 0, axis_index_groups=list(groups.values()), tiled=True
    )


def over_half(value):
    value = among(jnp.broadcast_to(value, (8, *value.shape)), "cells", 7).sum(axis=0)
    return among(jnp.broadcast_to(value, (4, *value.shape)), "cells", 24).sum(axis=0)


def split(value):
    upper = lax.reduce_precision(value, 8, 7)
    lower = lax.reduce_precision(value - upper, 8, 7)
    return upper.astype(jnp.bfloat16), lower.astype(jnp.bfloat16)


def in_parts(left, upper, lower, dim):
    first, second = split(left)
    rank = left.shape[0]

    def dot(a, b):
        return lax.dot_general(a, b, (((1,), (dim,)), ((), ())), preferred_element_type=jnp.float32)

    wide = dot(jnp.concatenate([first, second]), upper)
    return wide[:rank] + (wide[rank:] + dot(first, lower))


def in_rows(value):
    return with_layout_constraint(value, Layout(major_to_minor=(0, 1)))


def gram_of(rows_t):
    return lax.dot_general(rows_t, rows_t, (((1,), (1,)), ((), ())), precision=highest)


def inverse_factor_kernel(gram_ref, out_ref):
    size = gram_ref.shape[0]
    tiles = size // 8
    lane = lax.broadcasted_iota(jnp.int32, (8, 2 * size), 1)
    line = lax.broadcasted_iota(jnp.int32, (8, 2 * size), 0)
    gram = gram_ref[...]
    both = jnp.concatenate([gram, jnp.zeros_like(gram)], axis=1)
    rows = [
        jnp.where(lane == line + (size + 8 * t), 1.0, both[8 * t : 8 * t + 8]) for t in range(tiles)
    ]
    for k in range(size):
        t, r = divmod(k, 8)
        columns = [
            jnp.broadcast_to(rows[u][:, k : k + 1], (8, 2 * size)) for u in range(t, tiles)
        ]
        unit = (rows[t] / columns[0])[r : r + 1]
        pivot = jnp.broadcast_to(unit, (8, 2 * size))
        for u in range(t, tiles):
            column = columns[u - t]
            if u == t:
                column = jnp.where(line > r, column, 0.0)
            rows[u] = rows[u] - column * pivot
    for t in range(tiles):
        diagonal = jnp.sum(jnp.where(lane == line + 8 * t, rows[t], 0.0), axis=1, keepdims=True)
        out_ref[8 * t : 8 * t + 8] = rows[t][:, size:] / jnp.sqrt(diagonal)


def inverse_factor(gram):
    return pl.pallas_call(
        inverse_factor_kernel,
        out_shape=jax.ShapeDtypeStruct(gram.shape, gram.dtype),
        in_specs=[pl.BlockSpec(memory_space=pltpu.VMEM)],
        out_specs=pl.BlockSpec(memory_space=pltpu.VMEM),
        compiler_params=pltpu.CompilerParams(vmem_limit_bytes=1 << 20),
        cost_estimate=pl.CostEstimate(flops=1 << 20, bytes_accessed=1 << 15, transcendentals=128),
        name="inverse_factor",
    )(gram)


def shards(counts, start_basis):
    genes_dev, cells_dev = counts.shape
    rank = start_basis.shape[1]
    half_devs = lax.axis_size("cells") // 2
    set_cells = cells_dev * half_devs
    share = cells_dev // lax.axis_size("genes")
    core = lax.axis_index("genes") % 2
    side = lax.axis_index("genes") // 2

    raw_counts = counts.astype(jnp.float32)
    totals = lax.all_gather(jnp.sum(raw_counts, axis=0)[None], "genes", tiled=True).sum(axis=0)
    per_cell = 10000.0 / totals
    lognorm = jnp.log(1.0 + raw_counts * per_cell[None, :])

    sums = jnp.stack([jnp.sum(lognorm, axis=1), jnp.sum(lognorm * lognorm, axis=1)])
    sums = over_half(sums)
    center = sums[0] / set_cells
    spread = sums[1] / set_cells - center * center
    scale = 1.0 / jnp.sqrt(spread + epsilon)

    def scaled_parts(chunk, center, scale):
        cells = slice(2 * share * chunk, 2 * share * (chunk + 1))
        kept = jnp.log(1.0 + counts[:, cells].astype(jnp.float32) * per_cell[None, cells])
        return split(jnp.minimum((kept - center[:, None]) * scale[:, None], clip_top))

    def project(weight_t, parts):
        return in_parts(weight_t, *parts, 0)

    def exchanged(first, second):
        mine = jnp.where(core == 0, first, second)
        sent = jnp.where(core == 0, second, first)
        return mine + swapped(sent, "genes", 1)

    def product(partial):
        quarter = rank // 4
        part = among(in_rows(partial).reshape(4, quarter, genes_dev), "cells", 3).sum(axis=0)
        part = part + swapped(part, "cells", 4)
        came = [swapped(part, "cells", half_devs | mask) for mask in (0, 8, 16, 24)]
        part = (came[0] + came[1]) + (came[2] + came[3])
        return among(jnp.broadcast_to(part, (4, *part.shape)), "cells", 3).reshape(rank, genes_dev)

    def on_cores(partial):
        return exchanged(partial[:, :share], partial[:, share:])

    def whole(half):
        twin = swapped(half, "genes", 1)
        first, second = jnp.where(core == 0, half, twin), jnp.where(core == 0, twin, half)
        return jnp.concatenate([first, second], axis=1)

    weight_t = start_basis.T
    front = scaled_parts(0, center, scale)
    first = on_cores(project(weight_t, front))
    center, scale, first = lax.optimization_barrier((center, scale, first))
    theirs = swapped(first, "genes", 2)
    first = first + theirs
    back = scaled_parts(1, center, scale)
    partial = project(weight_t, back)
    second = on_cores(partial)
    theirs = swapped(second, "genes", 2)
    second = second + theirs
    partial = in_parts(whole(first), *front, 1)
    weight_t = product(partial + in_parts(whole(second), *back, 1))

    weight_t, gram = lax.optimization_barrier((weight_t, gram_of(weight_t)))
    gram = over_four(gram, "genes", 1, 2)
    partial = project(weight_t, front)
    first = on_cores(partial)
    first, weight_t = lax.optimization_barrier((first, weight_t))
    theirs = swapped(first, "genes", 2)
    first = first + theirs
    partial = project(weight_t, back)
    second = on_cores(partial)
    second, gram = lax.optimization_barrier((second, gram))
    inverse = inverse_factor(gram)
    theirs = swapped(second, "genes", 2)
    second = second + theirs
    first = whole(jnp.dot(inverse, first, precision=highest))
    second = whole(jnp.dot(inverse, second, precision=highest))
    partial = in_parts(first, *front, 1)
    weight_t = product(partial + in_parts(second, *back, 1))

    weight_t, gram = lax.optimization_barrier((weight_t, gram_of(weight_t)))
    gram = over_four(gram, "genes", 1, 2)
    first, second = project(weight_t, front), project(weight_t, back)
    half = exchanged(
        jnp.concatenate([first[:, :share], second[:, :share]], axis=1),
        jnp.concatenate([first[:, share:], second[:, share:]], axis=1),
    )
    half, gram = lax.optimization_barrier((half, gram))
    inverse = inverse_factor(gram)
    mine = jnp.where(side == 0, half[:, :share], half[:, share:])
    sent = jnp.where(side == 0, half[:, share:], half[:, :share])
    rows = jnp.dot(inverse, mine + swapped(sent, "genes", 2), precision=highest)
    gram = over_half(over_four(gram_of(rows), "genes", 1, 2))
    final = jnp.dot(inverse_factor(gram), rows, precision=highest)
    return final.T * math.sqrt(set_cells)


def solution(mesh):
    placed = (P("genes", "cells"), P("genes", None))
    return jax.shard_map(
        shards, mesh=mesh, in_specs=placed, out_specs=P(("cells", "genes"), None), check_vma=False
    )
```

```python
import math

import jax
import jax.numpy as jnp
from jax import lax
from jax.experimental import pallas as pl
from jax.experimental.layout import Layout, with_layout_constraint
from jax.experimental.pallas import tpu as pltpu
from jax.sharding import PartitionSpec as P


epsilon = 1e-05
clip_top = 10.0
highest = lax.Precision.HIGHEST


def swapped(value, axis, mask):
    return lax.ppermute(value, axis, [(s, s ^ mask) for s in range(lax.axis_size(axis))])


def over_four(value, axis, low, high):
    first = value + swapped(value, axis, low)
    return first + (swapped(value, axis, high) + swapped(value, axis, low | high))


def over_half(value):
    value = over_four(value, "cells", 1, 2)
    value = over_four(value, "cells", 8, 16)
    return value + swapped(value, "cells", 4)


def split(value):
    upper = lax.reduce_precision(value, 8, 7)
    lower = lax.reduce_precision(value - upper, 8, 7)
    return upper.astype(jnp.bfloat16), lower.astype(jnp.bfloat16)


def in_parts(left, upper, lower, dim):
    first, second = split(left)
    rank = left.shape[0]

    def dot(a, b):
        return lax.dot_general(a, b, (((1,), (dim,)), ((), ())), preferred_element_type=jnp.float32)

    wide = dot(jnp.concatenate([first, second]), upper)
    return wide[:rank] + (wide[rank:] + dot(first, lower))


def in_rows(value):
    return with_layout_constraint(value, Layout(major_to_minor=(0, 1)))


def gram_of(rows_t):
    return lax.dot_general(rows_t, rows_t, (((1,), (1,)), ((), ())), precision=highest)


def inverse_factor_kernel(gram_ref, out_ref):
    size = gram_ref.shape[0]
    tiles = size // 8
    lane = lax.broadcasted_iota(jnp.int32, (8, 2 * size), 1)
    line = lax.broadcasted_iota(jnp.int32, (8, 2 * size), 0)
    gram = gram_ref[...]
    both = jnp.concatenate([gram, jnp.zeros_like(gram)], axis=1)
    rows = [
        jnp.where(lane == line + (size + 8 * t), 1.0, both[8 * t : 8 * t + 8]) for t in range(tiles)
    ]
    for k in range(size):
        t, r = divmod(k, 8)
        columns = [
            jnp.broadcast_to(rows[u][:, k : k + 1], (8, 2 * size)) for u in range(t, tiles)
        ]
        unit = (rows[t] / columns[0])[r : r + 1]
        pivot = jnp.broadcast_to(unit, (8, 2 * size))
        for u in range(t, tiles):
            column = columns[u - t]
            if u == t:
                column = jnp.where(line > r, column, 0.0)
            rows[u] = rows[u] - column * pivot
    for t in range(tiles):
        diagonal = jnp.sum(jnp.where(lane == line + 8 * t, rows[t], 0.0), axis=1, keepdims=True)
        out_ref[8 * t : 8 * t + 8] = rows[t][:, size:] / jnp.sqrt(diagonal)


def inverse_factor(gram):
    return pl.pallas_call(
        inverse_factor_kernel,
        out_shape=jax.ShapeDtypeStruct(gram.shape, gram.dtype),
        in_specs=[pl.BlockSpec(memory_space=pltpu.VMEM)],
        out_specs=pl.BlockSpec(memory_space=pltpu.VMEM),
        compiler_params=pltpu.CompilerParams(vmem_limit_bytes=1 << 20),
        cost_estimate=pl.CostEstimate(flops=1 << 20, bytes_accessed=1 << 15, transcendentals=128),
        name="inverse_factor",
    )(gram)


def shards(counts, start_basis):
    _, cells_dev = counts.shape
    rank = start_basis.shape[1]
    half_devs = lax.axis_size("cells") // 2
    set_cells = cells_dev * half_devs
    share = cells_dev // lax.axis_size("genes")
    core = lax.axis_index("genes") % 2
    side = lax.axis_index("genes") // 2

    raw_counts = counts.astype(jnp.float32)
    totals = lax.all_gather(jnp.sum(raw_counts, axis=0)[None], "genes", tiled=True).sum(axis=0)
    per_cell = 10000.0 / totals
    lognorm = jnp.log(1.0 + raw_counts * per_cell[None, :])

    sums = jnp.stack([jnp.sum(lognorm, axis=1), jnp.sum(lognorm * lognorm, axis=1)])
    sums = over_half(sums)
    center = sums[0] / set_cells
    spread = sums[1] / set_cells - center * center
    scale = 1.0 / jnp.sqrt(spread + epsilon)

    def scaled_parts(chunk, center, scale):
        cells = slice(2 * share * chunk, 2 * share * (chunk + 1))
        kept = jnp.log(1.0 + counts[:, cells].astype(jnp.float32) * per_cell[None, cells])
        return split(jnp.minimum((kept - center[:, None]) * scale[:, None], clip_top))

    def project(weight_t, parts):
        return in_parts(weight_t, *parts, 0)

    def exchanged(first, second):
        mine = jnp.where(core == 0, first, second)
        sent = jnp.where(core == 0, second, first)
        return mine + swapped(sent, "genes", 1)

    place = lax.axis_index("cells") % 4
    low, high = place % 2 == 1, place // 2 == 1

    def crossed(pieces):
        a, b, c, d = pieces
        a, b, c, d = jnp.where(low, b, a), jnp.where(low, a, b), jnp.where(low, d, c), jnp.where(low, c, d)
        return jnp.where(high, c, a), jnp.where(high, d, b), jnp.where(high, a, c), jnp.where(high, b, d)

    def product(partial):
        partial = in_rows(partial)
        quarter = rank // 4
        kept, *sent = crossed([partial[i * quarter : (i + 1) * quarter] for i in range(4)])
        came = [swapped(piece, "cells", i + 1) for i, piece in enumerate(sent)]
        part = (kept + came[0]) + (came[1] + came[2])
        part = part + swapped(part, "cells", 4)
        came = [swapped(part, "cells", half_devs | mask) for mask in (0, 8, 16, 24)]
        part = (came[0] + came[1]) + (came[2] + came[3])
        came = [swapped(part, "cells", i) for i in (1, 2, 3)]
        return in_rows(jnp.concatenate(crossed([part, *came])))

    def on_cores(partial):
        return exchanged(partial[:, :share], partial[:, share:])

    def whole(half):
        twin = swapped(half, "genes", 1)
        first, second = jnp.where(core == 0, half, twin), jnp.where(core == 0, twin, half)
        return jnp.concatenate([first, second], axis=1)

    weight_t = start_basis.T
    front = scaled_parts(0, center, scale)
    first = on_cores(project(weight_t, front))
    center, scale, first = lax.optimization_barrier((center, scale, first))
    theirs = swapped(first, "genes", 2)
    first = first + theirs
    back = scaled_parts(1, center, scale)
    partial = project(weight_t, back)
    second = on_cores(partial)
    theirs = swapped(second, "genes", 2)
    second = second + theirs
    partial = in_parts(whole(first), *front, 1)
    weight_t = product(partial + in_parts(whole(second), *back, 1))

    weight_t, gram = lax.optimization_barrier((weight_t, gram_of(weight_t)))
    gram = over_four(gram, "genes", 1, 2)
    partial = project(weight_t, front)
    first = on_cores(partial)
    first, weight_t = lax.optimization_barrier((first, weight_t))
    theirs = swapped(first, "genes", 2)
    first = first + theirs
    partial = project(weight_t, back)
    second = on_cores(partial)
    second, gram = lax.optimization_barrier((second, gram))
    inverse = inverse_factor(gram)
    theirs = swapped(second, "genes", 2)
    second = second + theirs
    first = whole(jnp.dot(inverse, first, precision=highest))
    second = whole(jnp.dot(inverse, second, precision=highest))
    partial = in_parts(first, *front, 1)
    weight_t = product(partial + in_parts(second, *back, 1))

    weight_t, gram = lax.optimization_barrier((weight_t, gram_of(weight_t)))
    gram = over_four(gram, "genes", 1, 2)
    first, second = project(weight_t, front), project(weight_t, back)
    half = exchanged(
        jnp.concatenate([first[:, :share], second[:, :share]], axis=1),
        jnp.concatenate([first[:, share:], second[:, share:]], axis=1),
    )
    half, gram = lax.optimization_barrier((half, gram))
    inverse = inverse_factor(gram)
    mine = jnp.where(side == 0, half[:, :share], half[:, share:])
    sent = jnp.where(side == 0, half[:, share:], half[:, :share])
    rows = jnp.dot(inverse, mine + swapped(sent, "genes", 2), precision=highest)
    gram = over_half(over_four(gram_of(rows), "genes", 1, 2))
    final = jnp.dot(inverse_factor(gram), rows, precision=highest)
    return final.T * math.sqrt(set_cells)


def solution(mesh):
    placed = (P("genes", "cells"), P("genes", None))
    return jax.shard_map(
        shards, mesh=mesh, in_specs=placed, out_specs=P(("cells", "genes"), None), check_vma=False
    )
```
